32 devices in a mesh: row: 16 (over z, x, core), col: 2 (over y).
Axes of the slice: x: 2, y: 2, z: 4, core: 2. Of those that a mesh axis runs over, the one named last changes fastest.
Arguments:
- row_features: bfloat16 [256, 256], P(('row', 'col')), may hold values from -6 to 6
- col_features: bfloat16 [512, 256], P(('col', 'row')), may hold values from -6 to 6
- row_proj: bfloat16 [256, 64], replicated, may hold values from -0.375 to 0.375
- col_proj: bfloat16 [256, 64], replicated, may hold values from -0.375 to 0.375
- pair_weight: bfloat16 [2, 3, 3, 64, 64], replicated, may hold values from -0.1875 to 0.1875
- pair_bias: float32 [64], replicated, may hold values from -4 to 4
- conv_weight: bfloat16 [3, 3, 64, 64], replicated, may hold values from -0.25 to 0.25
- dilations: int32 [2], replicated, may hold values from 1 to 8, as said below
- cotangent: bfloat16 [64, 256, 512], P(None, 'row', 'col'), may hold values from -6 to 6
Outputs:
- pair_out: bfloat16 [64, 256, 512], P(None, 'row', 'col')
- grad_row_features: float32 [256, 256], P(('row', 'col'))
- grad_col_features: float32 [512, 256], P(('col', 'row'))
- grad_row_proj: float32 [256, 64], replicated
- grad_col_proj: float32 [256, 64], replicated
- grad_pair_weight: float32 [2, 3, 3, 64, 64], replicated
- grad_pair_bias: float32 [64], replicated
- grad_conv_weight: float32 [3, 3, 64, 64], replicated
The draws below stay inside these ranges and needn't reach their ends.
Inputs may be any that keep to these rules, and one draw needn't show every extreme that they name: One of the two dilations equals 8.
All inputs are finite; a program needn't handle non-finite values.
Results may differ from the reference program's by a relative error of at most 0.0054.
Values may be sent and summed in bfloat16 or wider, within the bound.
No kernel may reach another device: no remote copies, remote signals or barrier semaphores. Data moves between devices by JAX's collectives and lax.ppermute only.
A program may use at most 64 MiB of HBM per device.

```python
import jax
import jax.numpy as jnp
from jax import lax

CHANNELS = 256
PAIR_CHANNELS = 64
MAX_DILATION = 8
ROW_DEV = 16
ROW_BINS = 256
COL_BINS = 512


def draw_dilations(key, part):
    rate_key, order_key = jax.random.split(jax.random.fold_in(key, 11))
    free_rate = jax.random.randint(rate_key, (), 1, MAX_DILATION + 1).astype(jnp.int32)
    order_bit = jax.random.randint(order_key, (), 0, 2).astype(jnp.int32)
    largest = jnp.full((), MAX_DILATION, jnp.int32)
    forward = jnp.stack([largest, free_rate])
    backward = jnp.stack([free_rate, largest])
    return jnp.where(order_bit == 1, backward, forward).astype(jnp.int32)


def steps_of(own_key, extent, pieces, least, high):
    def one(axis_at, blocks):
        heights = jax.random.uniform(jax.random.fold_in(jax.random.fold_in(own_key, 6), axis_at), (blocks,), jnp.float32, least / len(pieces), high / len(pieces))
        return jnp.repeat(jnp.exp(heights), extent[axis_at] // blocks).reshape((-1,) + (1,) * (len(extent) - axis_at - 1))

    gain = one(*pieces[0])
    for cut in pieces[1:]:
        gain = gain * one(*cut)
    return gain


def noise(rng, shape, spread, bound, cuts=(), kind=jnp.bfloat16):
    loudness = steps_of(rng, shape, cuts, -0.22, 0.18) if cuts else 1.0
    drawn = jax.random.normal(rng, shape, jnp.float32) * spread * loudness
    return jnp.minimum(jnp.maximum(drawn, -bound), bound).astype(kind)


def setup_inputs(seed: int = 0) -> dict:
    arg_keys = jax.random.split(jax.random.key(seed), 10)
    row_features = noise(arg_keys[0], (ROW_BINS, CHANNELS), 1.0, 6.0, ((0, 32),))
    col_features = noise(arg_keys[1], (COL_BINS, CHANNELS), 1.0, 6.0, ((0, 32),))
    row_proj = noise(arg_keys[2], (CHANNELS, PAIR_CHANNELS), CHANNELS ** -0.5, 0.375)
    col_proj = noise(arg_keys[3], (CHANNELS, PAIR_CHANNELS), CHANNELS ** -0.5, 0.375)
    pair_weight = noise(arg_keys[4], (2, 3, 3, PAIR_CHANNELS, PAIR_CHANNELS), (18 * PAIR_CHANNELS) ** -0.5, 0.1875)
    pair_bias = noise(arg_keys[5], (PAIR_CHANNELS,), 1.0, 4.0, (), jnp.float32)
    conv_weight = noise(arg_keys[6], (3, 3, PAIR_CHANNELS, PAIR_CHANNELS), (9 * PAIR_CHANNELS) ** -0.5, 0.25)
    dilations = draw_dilations(jax.random.fold_in(arg_keys[9], 71), 0)
    cotangent = noise(arg_keys[8], (PAIR_CHANNELS, ROW_BINS, COL_BINS), 1.0, 6.0, ((1, 16), (2, 2)))
    return dict(row_features=row_features, col_features=col_features, row_proj=row_proj, col_proj=col_proj, pair_weight=pair_weight, pair_bias=pair_bias, conv_weight=conv_weight, dilations=dilations, cotangent=cotangent)


def line_terms(padded, weights, dilation, count, offset):
    shifted = jnp.stack([lax.dynamic_slice_in_dim(padded, (offset + (tap_idx - 1) * dilation).astype(jnp.int32), count, 0) for tap_idx in range(3)])
    return jnp.einsum("kip,kqpo->qio", shifted.astype(jnp.float32), weights.astype(jnp.float32), precision=lax.Precision.HIGHEST)


def line_valid(first_cell, count, cell_limit, dilation):
    cells = first_cell + jnp.arange(count, dtype=jnp.int32)
    columns = [((cells + (tap_idx - 1) * dilation >= 0) & (cells + (tap_idx - 1) * dilation < cell_limit)) for tap_idx in range(3)]
    return jnp.stack(columns, axis=1).astype(jnp.float32)


def inside_mask(first_cell, count, cell_limit):
    cells = first_cell + jnp.arange(count, dtype=jnp.int32)
    return ((cells >= 0) & (cells < cell_limit)).astype(jnp.float32)


def pair_field(row_terms, col_terms, row_valid, col_valid, bias):
    from_rows = jnp.einsum("jq,qic->cij", col_valid, row_terms, precision=lax.Precision.HIGHEST)
    from_cols = jnp.einsum("ik,kjc->cij", row_valid, col_terms, precision=lax.Precision.HIGHEST)
    return from_rows + from_cols + bias[:, None, None]


def window_at(padded, row_index, col_index, rows, cols):
    anchor = jnp.zeros((), jnp.int32)
    return lax.dynamic_slice(padded, (anchor, row_index.astype(jnp.int32), col_index.astype(jnp.int32)), (padded.shape[0], rows, cols))


def conv_taps(padded, weight, dilation, rows, cols, margin):
    result = jnp.zeros((weight.shape[3], rows, cols), jnp.float32)
    for tap_row in range(3):
        for tap_col in range(3):
            window = window_at(padded, margin + (tap_row - 1) * dilation, margin + (tap_col - 1) * dilation, rows, cols)
            result = result + jnp.einsum("co,cij->oij", weight[tap_row, tap_col].astype(jnp.float32), window.astype(jnp.float32), precision=lax.Precision.HIGHEST)
    return result


def back_taps(padded, weight, dilation, rows, cols, margin):
    result = jnp.zeros((weight.shape[2], rows, cols), jnp.float32)
    for tap_row in range(3):
        for tap_col in range(3):
            window = window_at(padded, margin - (tap_row - 1) * dilation, margin - (tap_col - 1) * dilation, rows, cols)
            result = result + jnp.einsum("co,oij->cij", weight[tap_row, tap_col].astype(jnp.float32), window.astype(jnp.float32), precision=lax.Precision.HIGHEST)
    return result


def tap_grads(hidden_pad, grads, dilation, rows, cols, margin):
    stacked = []
    for tap_row in range(3):
        line_list = []
        for tap_col in range(3):
            window = window_at(hidden_pad, margin + (tap_row - 1) * dilation, margin + (tap_col - 1) * dilation, rows, cols)
            line_list.append(jnp.einsum("cij,oij->co", window.astype(jnp.float32), grads.astype(jnp.float32), precision=lax.Precision.HIGHEST))
        stacked.append(jnp.stack(line_list))
    return jnp.stack(stacked)


def reference(row_features, col_features, row_proj, col_proj, pair_weight, pair_bias, conv_weight, dilations, cotangent):
    first_rate = dilations[0]
    second_rate = dilations[1]
    margin = MAX_DILATION
    wide_pad = 2 * MAX_DILATION
    width = PAIR_CHANNELS
    rows_a = jnp.dot(row_features, row_proj, preferred_element_type=jnp.float32).astype(jnp.bfloat16)
    cols_b = jnp.dot(col_features, col_proj, preferred_element_type=jnp.float32).astype(jnp.bfloat16)
    a_pad = jnp.pad(rows_a, ((wide_pad, wide_pad), (0, 0)))
    b_pad = jnp.pad(cols_b, ((wide_pad, wide_pad), (0, 0)))
    row_terms = line_terms(a_pad, pair_weight[0], first_rate, ROW_BINS + 2 * margin, margin)
    col_terms = line_terms(b_pad, jnp.swapaxes(pair_weight[1], 0, 1), first_rate, COL_BINS + 2 * margin, margin)
    row_valid = line_valid(-margin, ROW_BINS + 2 * margin, ROW_BINS, first_rate)
    col_valid = line_valid(-margin, COL_BINS + 2 * margin, COL_BINS, first_rate)
    row_inside = inside_mask(-margin, ROW_BINS + 2 * margin, ROW_BINS)
    col_inside = inside_mask(-margin, COL_BINS + 2 * margin, COL_BINS)
    grad_pad = jnp.pad(cotangent, ((0, 0), (margin, margin), (margin, margin)))
    block_rows = ROW_DEV
    block_count = ROW_BINS // block_rows
    col_valid_own = col_valid[margin:margin + COL_BINS]

    def one_block(carry, block_index):
        conv_grad, bias_grad, col_sums = carry
        start_row = block_index * block_rows
        terms_here = lax.dynamic_slice_in_dim(row_terms, start_row, block_rows + 2 * margin, 1)
        valid_here = lax.dynamic_slice_in_dim(row_valid, start_row, block_rows + 2 * margin, 0)
        inside_here = lax.dynamic_slice_in_dim(row_inside, start_row, block_rows + 2 * margin, 0)
        pre_act = pair_field(terms_here, col_terms, valid_here, col_valid, pair_bias)
        hidden = (jax.nn.silu(pre_act) * inside_here[None, :, None] * col_inside[None, None, :]).astype(jnp.bfloat16)
        conv_mixed = conv_taps(hidden, conv_weight, second_rate, block_rows, COL_BINS, margin)
        hidden_own = hidden[:, margin:margin + block_rows, margin:margin + COL_BINS]
        output = (hidden_own.astype(jnp.float32) + conv_mixed).astype(jnp.bfloat16)
        grad_here = lax.dynamic_slice_in_dim(grad_pad, start_row, block_rows + 2 * margin, 1)
        grad_own = grad_here[:, margin:margin + block_rows, margin:margin + COL_BINS]
        d_hidden = grad_own.astype(jnp.float32) + back_taps(grad_here, conv_weight, second_rate, block_rows, COL_BINS, margin)
        conv_grad = conv_grad + tap_grads(hidden, grad_own, second_rate, block_rows, COL_BINS, margin)
        pre_own = pre_act[:, margin:margin + block_rows, margin:margin + COL_BINS]
        sigmoid_own = jax.nn.sigmoid(pre_own)
        d_wide = d_hidden * sigmoid_own * (1.0 + pre_own * (1.0 - sigmoid_own))
        bias_grad = bias_grad + jnp.sum(d_wide, axis=(1, 2))
        row_valid_own = valid_here[margin:margin + block_rows]
        row_part = jnp.einsum("jq,cij->qic", col_valid_own, d_wide, precision=lax.Precision.HIGHEST)
        col_sums = col_sums + jnp.einsum("ik,cij->kjc", row_valid_own, d_wide, precision=lax.Precision.HIGHEST)
        return (conv_grad, bias_grad, col_sums), (output, row_part)

    start_carry = (jnp.zeros((3, 3, width, width), jnp.float32), jnp.zeros((width,), jnp.float32), jnp.zeros((3, COL_BINS, width), jnp.float32))
    (conv_grad, bias_grad, col_sums), (outputs, row_parts) = lax.scan(one_block, start_carry, jnp.arange(block_count, dtype=jnp.int32))
    pair_out = jnp.moveaxis(outputs, 0, 1).reshape(width, ROW_BINS, COL_BINS)
    row_sums = jnp.moveaxis(row_parts, 0, 1).reshape(3, ROW_BINS, width)
    back_rows = jnp.einsum("qio,kqpo->kip", row_sums, pair_weight[0].astype(jnp.float32), precision=lax.Precision.HIGHEST)
    back_cols = jnp.einsum("kjo,kqpo->qjp", col_sums, pair_weight[1].astype(jnp.float32), precision=lax.Precision.HIGHEST)
    rows_back_pad = jnp.pad(back_rows, ((0, 0), (margin, margin), (0, 0)))
    cols_back_pad = jnp.pad(back_cols, ((0, 0), (margin, margin), (0, 0)))
    d_rows = sum(lax.dynamic_slice_in_dim(rows_back_pad[tap_idx], (margin - (tap_idx - 1) * first_rate).astype(jnp.int32), ROW_BINS, 0) for tap_idx in range(3))
    d_cols = sum(lax.dynamic_slice_in_dim(cols_back_pad[tap_idx], (margin - (tap_idx - 1) * first_rate).astype(jnp.int32), COL_BINS, 0) for tap_idx in range(3))
    d_rows = d_rows.astype(jnp.bfloat16)
    d_cols = d_cols.astype(jnp.bfloat16)
    grad_row_features = jnp.dot(d_rows, row_proj.T, preferred_element_type=jnp.float32)
    grad_col_features = jnp.dot(d_cols, col_proj.T, preferred_element_type=jnp.float32)
    grad_row_proj = jnp.dot(row_features.T, d_rows, preferred_element_type=jnp.float32)
    grad_col_proj = jnp.dot(col_features.T, d_cols, preferred_element_type=jnp.float32)
    row_shifted = jnp.stack([lax.dynamic_slice_in_dim(a_pad, (wide_pad + (tap_idx - 1) * first_rate).astype(jnp.int32), ROW_BINS, 0) for tap_idx in range(3)])
    col_shifted = jnp.stack([lax.dynamic_slice_in_dim(b_pad, (wide_pad + (tap_idx - 1) * first_rate).astype(jnp.int32), COL_BINS, 0) for tap_idx in range(3)])
    grad_row_pair = jnp.einsum("kip,qio->kqpo", row_shifted.astype(jnp.float32), row_sums, precision=lax.Precision.HIGHEST)
    grad_col_pair = jnp.einsum("qjp,kjo->kqpo", col_shifted.astype(jnp.float32), col_sums, precision=lax.Precision.HIGHEST)
    grad_pair_weight = jnp.stack([grad_row_pair, grad_col_pair])
    return (pair_out, grad_row_features, grad_col_features, grad_row_proj, grad_col_proj, grad_pair_weight, bias_grad, conv_grad)
```

```python
import functools

import jax
import jax.numpy as jnp
from jax import lax
from jax.experimental import pallas as pl
from jax.experimental.pallas import tpu as pltpu
from jax.sharding import PartitionSpec as P

MAX_DILATION = 8
LANES = 128
ROW_LANES = 128
F32 = jnp.float32
BF16 = jnp.bfloat16
ALL = ("row", "col")
NT = (((1,), (1,)), ((), ()))
TN = (((0,), (0,)), ((), ()))
GRAD_ROWS = 864


def round_up(value, step):
    return (value + step - 1) // step * step


def mm(a, b):
    return jnp.dot(a, b, preferred_element_type=F32)


def mm_nt(a, b):
    return lax.dot_general(a, b, NT, preferred_element_type=F32)


def mm_tn(a, b):
    return lax.dot_general(a, b, TN, preferred_element_type=F32)


def split(value):
    high = value.astype(BF16)
    low = (value - high.astype(F32)).astype(BF16)
    return high, low


def call(kernel, outs, *args, scratch=(), flops=0, smem=(), mib=20):
    size = sum(a.size * a.dtype.itemsize for a in args)
    size += sum(o.size * o.dtype.itemsize for o in outs)
    specs = [
        pl.BlockSpec(memory_space=pltpu.SMEM if n in smem else pltpu.VMEM)
        for n in range(len(args))
    ]
    return pl.pallas_call(
        kernel,
        out_shape=tuple(outs),
        in_specs=specs,
        out_specs=tuple(pl.BlockSpec(memory_space=pltpu.VMEM) for _ in outs),
        scratch_shapes=list(scratch),
        compiler_params=pltpu.CompilerParams(vmem_limit_bytes=mib << 20),
        cost_estimate=pl.CostEstimate(flops=flops, bytes_accessed=size, transcendentals=0),
    )(*args)


def project_kernel(rf_ref, cf_ref, rp_ref, cp_ref, send_ref):
    devices, chunk, _ = send_ref.shape
    rows = mm(rf_ref[...], rp_ref[...])
    cols = mm(cf_ref[...], cp_ref[...])
    rows = jnp.concatenate([rows, jnp.zeros((chunk - rows.shape[0], 64), F32)], axis=0)
    if cols.shape[0] < chunk:
        cols = jnp.concatenate([cols, jnp.zeros((chunk - cols.shape[0], 64), F32)], axis=0)
    block = jnp.concatenate([cols, rows], axis=1).astype(BF16)

    def put(t, _):
        send_ref[t] = block
        return 0

    lax.fori_loop(0, devices, put, 0)


def back_kernel(dil_ref, cot_ref, weight_ref, rf_ref, cf_ref, dh_ref, shift_ref, feat_ref):
    rate = dil_ref[1]
    rows_here, channels, cols_here = cot_ref.shape
    wide = dh_ref.shape[2]
    margin = MAX_DILATION

    def clear(e, _):
        dh_ref[e] = jnp.zeros((channels, wide), F32)
        return 0

    lax.fori_loop(0, dh_ref.shape[0], clear, 0)
    weight = weight_ref[...]

    def one_row(i, _):
        own = cot_ref[i].astype(F32)
        own = jnp.concatenate([own, jnp.zeros((channels, wide - cols_here), F32)], axis=1)
        left = pltpu.roll(own, wide - rate, 1)
        right = pltpu.roll(own, rate, 1)
        taps = jnp.concatenate([left, own, right], axis=0).astype(BF16)
        shift_ref[i] = taps
        result = mm(weight, taps)
        dh_ref[margin + i - rate] += result[:channels]
        dh_ref[margin + i] += result[channels : 2 * channels] + own
        dh_ref[margin + i + rate] += result[2 * channels :]
        return 0

    lax.fori_loop(0, rows_here, one_row, 0)
    devices, chunk, _ = feat_ref.shape
    rf = rf_ref[...].astype(F32)
    cf = cf_ref[...].astype(F32)
    parts = [rf[:, :LANES], rf[:, LANES:], cf[:, :LANES], cf[:, LANES:]]
    used = sum(p.shape[0] for p in parts)
    if used < chunk:
        parts.append(jnp.zeros((chunk - used, LANES), F32))
    block = jnp.concatenate(parts, axis=0).astype(BF16)

    def put(t, _):
        feat_ref[t] = block
        return 0

    lax.fori_loop(0, devices, put, 0)


def line_taps(line, rate, wide):
    return jnp.concatenate(
        [pltpu.roll(line, rate, 1), line, pltpu.roll(line, wide - rate, 1)], axis=0
    )


def line_back(weight, sums, taps, rate, wide):
    high, low = split(sums)
    back = mm(weight, high) + mm(weight, low)
    n = back.shape[0] // 3
    line = pltpu.roll(back[:n], wide - rate, 1) + back[n : 2 * n]
    line = line + pltpu.roll(back[2 * n :], rate, 1)
    return line, mm_nt(taps, high) + mm_nt(taps, low)


def main_kernel(
    nr, nc, rp, cp, limits,
    dil_ref, recv_ref, wr_ref, wc_ref, bias_ref, dh_ref, shift_ref,
    hidden_ref, send_ref,
    bp_ref, ap_ref, rt_ref, rs_ref, cs_ref, grad_ref, dr_ref, dc_ref, pack_ref,
):
    d1 = dil_ref[0]
    d2 = dil_ref[1]
    r = lax.axis_index("row")
    c = lax.axis_index("col")
    rows_here, cols_here = limits
    ext, channels, wide = dh_ref.shape
    margin = MAX_DILATION
    halo = 2 * margin
    devices = nr * nc
    row_limit = rows_here * nr
    col_limit = cols_here * nc

    bp_ref[...] = jnp.zeros_like(bp_ref)
    ap_ref[...] = jnp.zeros_like(ap_ref)
    for n in range((cols_here + 2 * halo) // cp):
        piece = c * (cols_here // cp) - halo // cp + n
        safe = jnp.clip(piece, 0, devices - 1)
        src = lax.rem(safe, nr) * nc + safe // nr
        scale = jnp.where(piece == safe, 1.0, 0.0).astype(F32)
        at = (n * cp - halo) % wide
        bp_ref[at : at + cp, :] = recv_ref[src].astype(F32)[:cp] * scale
    for n in range((rows_here + 2 * halo) // rp):
        piece = r * (rows_here // rp) - halo // rp + n
        safe = jnp.clip(piece, 0, devices - 1)
        scale = jnp.where(piece == safe, 1.0, 0.0).astype(F32)
        at = (n * rp - halo) % ROW_LANES
        ap_ref[at : at + rp, :] = recv_ref[safe].astype(F32)[:rp] * scale
    b_line = bp_ref[...].T[:channels]
    a_line = ap_ref[...].T[channels:]
    b_taps = line_taps(b_line, d1, wide).astype(BF16)
    a_taps = line_taps(a_line, d1, ROW_LANES).astype(BF16)
    col_terms = mm_tn(wc_ref[...], b_taps)
    row_terms = mm_tn(wr_ref[...], a_taps)
    bias = jnp.broadcast_to(bias_ref[...], (8, LANES)).T[:channels, :1]
    row_terms = jnp.concatenate(
        [
            row_terms[:channels],
            row_terms[channels : 2 * channels] + bias,
            row_terms[2 * channels :],
        ],
        axis=0,
    )
    groups = ext // 8
    for g in range(groups):
        rt_ref[g] = pltpu.roll(row_terms, (margin - 8 * g) % ROW_LANES, 1)

    lane = lax.broadcasted_iota(jnp.int32, (8, wide), 1)[:1]
    place = jnp.where(lane < cols_here + (wide - cols_here) // 2, lane, lane - wide)
    cell = c * cols_here + place
    near = (place >= -margin) & (place < cols_here + margin)
    col_in = jnp.where(near & (cell >= 0) & (cell < col_limit), 1.0, 0.0).astype(F32)
    cv0 = jnp.where(cell - d1 >= 0, 1.0, 0.0).astype(F32)
    cv2 = jnp.where(cell + d1 < col_limit, 1.0, 0.0).astype(F32)
    cs_ref[...] = jnp.zeros_like(cs_ref)
    mark = lax.broadcasted_iota(jnp.int32, (channels, ROW_LANES), 1)
    ct = [col_terms[k * channels : (k + 1) * channels] for k in range(3)]

    def group(g, _):
        terms = rt_ref[g]
        acc = [jnp.zeros((channels, ROW_LANES), F32) for _ in range(3)]
        for u in range(8):
            e = g * 8 + u
            cell_row = r * rows_here + e - margin
            inside = jnp.where((cell_row >= 0) & (cell_row < row_limit), 1.0, 0.0).astype(F32)
            rv0 = jnp.where(cell_row - d1 >= 0, 1.0, 0.0).astype(F32)
            rv2 = jnp.where(cell_row + d1 < row_limit, 1.0, 0.0).astype(F32)
            rt = [terms[k * channels : (k + 1) * channels, u : u + 1] for k in range(3)]
            total = [None, None, None]
            hid = []
            for t in range(wide // LANES):
                s = slice(t * LANES, (t + 1) * LANES)
                pre = ct[1][:, s] + rv0 * ct[0][:, s] + rv2 * ct[2][:, s]
                pre = pre + rt[1] + cv0[:, s] * rt[0] + cv2[:, s] * rt[2]
                sig = 0.5 + 0.5 * jnp.tanh(0.5 * pre)
                mask = col_in[:, s] * inside
                hid.append(((pre * sig) * mask).astype(BF16))
                d = dh_ref[e, :, s] * (sig * (1.0 + pre * (1.0 - sig)) * mask)
                cs_ref[0:channels, s] += rv0 * d
                cs_ref[channels : 2 * channels, s] += d
                cs_ref[2 * channels : 3 * channels, s] += rv2 * d
                part = [d * cv0[:, s], d, d * cv2[:, s]]
                total = [p if o is None else o + p for o, p in zip(total, part)]
            hidden_ref[e] = jnp.concatenate(hid, axis=1)
            for q in range(3):
                line = jnp.sum(total[q], axis=1, keepdims=True)
                acc[q] = jnp.where(mark == u, line, acc[q])
        rs_ref[g] = jnp.concatenate(acc, axis=0)
        return 0

    lax.fori_loop(0, groups, group, 0)

    row_sums = pltpu.roll(rs_ref[0], ROW_LANES - margin, 1)
    for g in range(1, groups):
        row_sums = row_sums + pltpu.roll(rs_ref[g], (8 * g - margin) % ROW_LANES, 1)
    col_sums = cs_ref[...]
    bias_grad = jnp.sum(row_sums[channels : 2 * channels], axis=1, keepdims=True)
    row_line, row_grad = line_back(wr_ref[...], row_sums, a_taps, d1, ROW_LANES)
    col_line, col_grad = line_back(wc_ref[...], col_sums, b_taps, d1, wide)

    conv_grad = jnp.zeros((3 * channels, 3 * channels), F32)
    for i in range(rows_here):
        taps = jnp.concatenate(
            [
                hidden_ref[margin + i - d2],
                hidden_ref[margin + i],
                hidden_ref[margin + i + d2],
            ],
            axis=0,
        )
        conv_grad = conv_grad + mm_nt(taps, shift_ref[i])

    side = 3 * channels
    if grad_ref.shape[0] > GRAD_ROWS:
        grad_ref[GRAD_ROWS:, :] = jnp.zeros((grad_ref.shape[0] - GRAD_ROWS, LANES), F32)
    for n, grad in enumerate((row_grad, col_grad, conv_grad)):
        grad_ref[n * side : (n + 1) * side, :] = grad[:, :LANES]
    grad_ref[3 * side : 4 * side, :64] = row_grad[:, LANES:]
    grad_ref[3 * side : 4 * side, 64:] = col_grad[:, LANES:]
    grad_ref[4 * side : 4 * side + side // 2, :64] = conv_grad[: side // 2, LANES:]
    grad_ref[4 * side : 4 * side + side // 2, 64:] = conv_grad[side // 2 :, LANES:]

    def upright(line):
        n = line.shape[1]
        return jnp.concatenate([line, jnp.zeros((LANES - channels, n), F32)], axis=0).T

    dr = upright(row_line)
    dc = upright(col_line)
    dr_ref[...] = jnp.zeros_like(dr_ref)
    dc_ref[...] = jnp.zeros_like(dc_ref)
    base = pl.multiple_of(r * rows_here, 8)
    dr_ref[pl.ds(base, halo), :] = dr[ROW_LANES - halo :]
    dr_ref[pl.ds(base + halo, rows_here + halo), :] = dr[: rows_here + halo]
    base = pl.multiple_of(c * cols_here, 8)
    dc_ref[pl.ds(base, halo), :] = dc[wide - halo :]
    dc_ref[pl.ds(base + halo, cols_here + halo), :] = dc[: cols_here + halo]

    bias_row = jnp.broadcast_to(bias_grad, (channels, LANES)).T[:1]
    per = grad_ref.shape[0] // devices
    chunk = send_ref.shape[1]
    used = per + rp // 2 + cp // 2 + 1
    if used < chunk:
        pack_ref[used:, :] = jnp.zeros((chunk - used, LANES), F32)
    pack_ref[used - 1 : used, :64] = bias_row
    pack_ref[used - 1 : used, 64:] = jnp.zeros_like(bias_row)
    for t in range(devices):
        tr, tc = divmod(t, nc)
        pack_ref[:per, :] = grad_ref[t * per : (t + 1) * per, :]
        at = halo + t * rp
        pack_ref[per : per + rp // 2, :64] = dr_ref[at : at + rp // 2, :64]
        pack_ref[per : per + rp // 2, 64:] = dr_ref[at + rp // 2 : at + rp, :64]
        at = halo + tc * cols_here + tr * cp
        row = per + rp // 2
        pack_ref[row : row + cp // 2, :64] = dc_ref[at : at + cp // 2, :64]
        pack_ref[row : row + cp // 2, 64:] = dc_ref[at + cp // 2 : at + cp, :64]
        send_ref[t] = pack_ref[...].astype(BF16)


def forward_kernel(dil_ref, hidden_ref, weight_ref, out_ref, taps_ref):
    rate = dil_ref[1]
    rows_here, channels, cols_here = out_ref.shape
    wide = hidden_ref.shape[2]
    margin = MAX_DILATION

    def one_tap(e, _):
        own = hidden_ref[e].astype(F32)
        left = pltpu.roll(own, rate, 1)
        right = pltpu.roll(own, wide - rate, 1)
        taps = jnp.concatenate([left, own, right], axis=0)
        taps_ref[e] = taps[:, :cols_here].astype(BF16)
        return 0

    lax.fori_loop(0, hidden_ref.shape[0], one_tap, 0)
    weight = weight_ref[...]

    def one_row(i, _):
        taps = jnp.concatenate(
            [taps_ref[margin + i - rate], taps_ref[margin + i], taps_ref[margin + i + rate]],
            axis=0,
        )
        own = hidden_ref[margin + i].astype(F32)[:, :cols_here]
        out_ref[i] = (mm(weight, taps) + own).astype(BF16)
        return 0

    lax.fori_loop(0, rows_here, one_row, 0)


def sum_kernel(per, rp, cp, recv_ref, rproj_ref, cproj_ref, send_ref, bias_ref, gr_ref, gc_ref):
    devices = recv_ref.shape[0]

    total = recv_ref[0].astype(F32)
    for t in range(1, devices):
        total = total + recv_ref[t].astype(F32)
    block = total.astype(BF16)

    def put(t, _):
        send_ref[t] = block
        return 0

    lax.fori_loop(0, devices, put, 0)
    used = per + rp // 2 + cp // 2 + 1
    bias_ref[...] = total[used - 1 : used, :]
    dr = total[per : per + rp // 2]
    dc = total[per + rp // 2 : used - 1]
    dr = jnp.concatenate([dr[:, :64], dr[:, 64:]], axis=0).astype(BF16)
    dc = jnp.concatenate([dc[:, :64], dc[:, 64:]], axis=0).astype(BF16)
    gr_ref[...] = mm_nt(dr, rproj_ref[...])
    gc_ref[...] = mm_nt(dc, cproj_ref[...])


def final_kernel(
    per, rp, cp, recv_ref, feat_ref,
    grp_ref, gcp_ref, pair_ref, conv_ref,
    grad_ref, dr_ref, dc_ref, fr_ref, fc_ref,
):
    devices = recv_ref.shape[0]
    for t in range(devices):
        block = recv_ref[t].astype(F32)
        last = min((t + 1) * per, grad_ref.shape[0]) - t * per
        if last > 0:
            grad_ref[t * per : t * per + last, :] = block[:last]
        row = per
        dr_ref[t * rp : t * rp + rp // 2, :] = block[row : row + rp // 2, :64]
        dr_ref[t * rp + rp // 2 : (t + 1) * rp, :] = block[row : row + rp // 2, 64:]
        row = per + rp // 2
        dc_ref[t * cp : t * cp + cp // 2, :] = block[row : row + cp // 2, :64]
        dc_ref[t * cp + cp // 2 : (t + 1) * cp, :] = block[row : row + cp // 2, 64:]
        feat = feat_ref[t].astype(F32)
        fr_ref[t * rp : (t + 1) * rp, :LANES] = feat[:rp]
        fr_ref[t * rp : (t + 1) * rp, LANES:] = feat[rp : 2 * rp]
        row = 2 * rp
        fc_ref[t * cp : (t + 1) * cp, :LANES] = feat[row : row + cp]
        fc_ref[t * cp : (t + 1) * cp, LANES:] = feat[row + cp : row + 2 * cp]
    grp_ref[...] = mm_tn(fr_ref[...].astype(BF16), dr_ref[...].astype(BF16))
    gcp_ref[...] = mm_tn(fc_ref[...].astype(BF16), dc_ref[...].astype(BF16))
    n = 64
    side = 3 * n
    for k in range(3):
        for q in range(3):
            lanes = slice(0, 64) if q != 1 else slice(64, 128)
            at = n * k if q < 2 else 3 * side + n * k
            pair_ref[0, k, q] = grad_ref[at : at + n, lanes]
            lanes = slice(0, 64) if k == 0 else slice(64, 128)
            at = side + n * q if k < 2 else 3 * side + n * q
            pair_ref[1, k, q] = grad_ref[at : at + n, lanes]
            if q < 2:
                at = 2 * side + n * k
                lanes = slice(0, 64) if q == 0 else slice(64, 128)
                conv_ref[k, q] = grad_ref[at : at + n, lanes]
            else:
                at = 4 * side
                half = n // 2
                for h in range(2):
                    line = n * k + half * h
                    lanes = slice(0, 64) if line < side // 2 else slice(64, 128)
                    row = at + line % (side // 2)
                    conv_ref[k, q, half * h : half * (h + 1)] = grad_ref[row : row + half, lanes]


def exchange(value):
    return lax.all_to_all(value, ALL, 0, 0, tiled=True)


def shards(nr, nc, row_features, col_features, row_proj, col_proj, pair_weight, pair_bias,
           conv_weight, dilations, cotangent):
    devices = nr * nc
    channels, rows_here, cols_here = cotangent.shape
    rp, width = row_features.shape
    cp = col_features.shape[0]
    margin = MAX_DILATION
    ext = rows_here + 2 * margin
    wide = cols_here + LANES
    side = 3 * channels
    shape = jax.ShapeDtypeStruct

    chunk_a = round_up(max(rp, cp), 16)
    (line_send,) = call(
        project_kernel,
        [shape((devices, chunk_a, LANES), BF16)],
        row_features, col_features, row_proj, col_proj,
    )
    line_recv = exchange(line_send)

    back_weight = jnp.transpose(conv_weight, (0, 2, 1, 3)).reshape(side, side)
    front_weight = jnp.transpose(conv_weight, (3, 0, 1, 2)).reshape(channels, 3 * side)
    row_weight = jnp.transpose(pair_weight[0], (0, 2, 1, 3)).reshape(side, side)
    col_weight = jnp.transpose(pair_weight[1], (1, 2, 0, 3)).reshape(side, side)
    cot_rows = jnp.transpose(cotangent, (1, 0, 2))
    chunk_f = round_up(2 * rp + 2 * cp, 16)
    d_hidden, shifted, feat_send = call(
        back_kernel,
        [
            shape((ext, channels, wide), F32),
            shape((rows_here, side, wide), BF16),
            shape((devices, chunk_f, LANES), BF16),
        ],
        dilations, cot_rows, back_weight, row_features, col_features,
        smem=(0,), flops=2 * rows_here * side * side * wide,
    )
    feat_recv = exchange(feat_send)

    per = -(-GRAD_ROWS // devices)
    chunk_g = round_up(per + rp // 2 + cp // 2 + 1, 8)
    bias_in = jnp.concatenate([pair_bias, jnp.zeros((LANES - channels,), F32)]).reshape(1, LANES)
    hidden, grad_send = call(
        functools.partial(main_kernel, nr, nc, rp, cp, (rows_here, cols_here)),
        [shape((ext, channels, wide), BF16), shape((devices, chunk_g, LANES), BF16)],
        dilations, line_recv, row_weight, col_weight, bias_in, d_hidden, shifted,
        smem=(0,),
        flops=2 * rows_here * side * side * wide,
        scratch=[
            pltpu.VMEM((wide, LANES), F32),
            pltpu.VMEM((ROW_LANES, LANES), F32),
            pltpu.VMEM((ext // 8, side, ROW_LANES), F32),
            pltpu.VMEM((ext // 8, side, ROW_LANES), F32),
            pltpu.VMEM((side, wide), F32),
            pltpu.VMEM((per * devices, LANES), F32),
            pltpu.VMEM((devices * rp + 4 * margin, LANES), F32),
            pltpu.VMEM((devices * cp + 4 * margin, LANES), F32),
            pltpu.VMEM((chunk_g, LANES), F32),
        ],
    )
    grad_recv = exchange(grad_send)

    (out_rows,) = call(
        forward_kernel,
        [shape((rows_here, channels, cols_here), BF16)],
        dilations, hidden, front_weight,
        smem=(0,),
        flops=2 * rows_here * channels * 3 * side * cols_here,
        scratch=[pltpu.VMEM((ext, side, cols_here), BF16)],
    )
    pair_out = jnp.transpose(out_rows, (1, 0, 2))

    full_send, bias_row, grad_row_features, grad_col_features = call(
        functools.partial(sum_kernel, per, rp, cp),
        [
            shape((devices, chunk_g, LANES), BF16),
            shape((1, LANES), F32),
            shape((rp, width), F32),
            shape((cp, width), F32),
        ],
        grad_recv, row_proj, col_proj,
    )
    full_recv = exchange(full_send)
    grad_row_proj, grad_col_proj, grad_pair_weight, grad_conv_weight = call(
        functools.partial(final_kernel, per, rp, cp),
        [
            shape(row_proj.shape, F32),
            shape(col_proj.shape, F32),
            shape(pair_weight.shape, F32),
            shape(conv_weight.shape, F32),
        ],
        full_recv, feat_recv,
        scratch=[
            pltpu.VMEM((GRAD_ROWS, LANES), F32),
            pltpu.VMEM((devices * rp, channels), F32),
            pltpu.VMEM((devices * cp, channels), F32),
            pltpu.VMEM((devices * rp, width), F32),
            pltpu.VMEM((devices * cp, width), F32),
        ],
    )
    return (
        pair_out,
        grad_row_features,
        grad_col_features,
        grad_row_proj,
        grad_col_proj,
        grad_pair_weight,
        bias_row[0, :channels],
        grad_conv_weight,
    )


def solution(mesh):
    nr, nc = mesh.shape["row"], mesh.shape["col"]
    return jax.shard_map(
        functools.partial(shards, nr, nc),
        mesh=mesh,
        in_specs=(
            P(("row", "col"), None),
            P(("col", "row"), None),
            P(),
            P(),
            P(),
            P(),
            P(),
            P(),
            P(None, "row", "col"),
        ),
        out_specs=(
            P(None, "row", "col"),
            P(("row", "col"), None),
            P(("col", "row"), None),
            P(),
            P(),
            P(),
            P(),
            P(),
        ),
        check_vma=False,
    )
```
